32 devices in a mesh: grp: 2 (over x), pts: 16 (over z, y, core).
Axes of the slice: x: 2, y: 2, z: 4, core: 2. Of those that a mesh axis runs over, the one named last changes fastest.
Arguments:
- support: bfloat16 [4096, 64], P(('grp', 'pts')), parts along dimension 0, may hold values from -9 to 9
- clouds: bfloat16 [8, 4096, 64], P(None, ('grp', 'pts')), parts along dimension 1, may hold values from -6 to 6
- member_weights: float32 [16], P('grp'), parts along dimension 0, may hold values from 1 to 10
Outputs:
- new_support: float32 [4096, 64], P(('grp', 'pts')), parts along dimension 0
The draws below stay inside these ranges and needn't reach their ends.
There are 2 independent parts, one for each index of `grp`. The reference program is written for one: setup_inputs(seed, part) draws one part's arguments, and reference() takes and returns one part's arrays. A program takes and returns all parts, laid end to end along the dimension named above; each array names one. Nothing has to cross between parts.
All inputs are finite; a program needn't handle non-finite values.
Results may differ from the reference program's by a relative error of at most 0.001.
Values may be sent and summed in bfloat16 or wider, within the bound.
A program may use at most 128 MiB of HBM per device.

```python
import math
import jax
import jax.numpy as jnp
from jax import lax

DIM = 64
MEMB = 8
ITERS = 3
N = 2048
M = 2048


def draw_support(key, part):
    base_key = jax.random.fold_in(key, 11)
    level_key = jax.random.fold_in(key, 12)
    sign_key = jax.random.fold_in(key, 13)
    base = jnp.clip(jax.random.normal(base_key, (N, DIM), jnp.float32), -3.5, 3.5)
    level = jax.random.randint(level_key, (N,), 0, 8)
    strength = jnp.where(level == 5, 3.0, jnp.where(level == 6, 4.0, jnp.where(level == 7, 5.0, 0.0)))
    signs = (2 * jax.random.randint(sign_key, (DIM,), 0, 2) - 1).astype(jnp.float32)
    values = base + strength[:, None] * signs[None, :]
    return jnp.clip(values, -9.0, 9.0).astype(jnp.bfloat16)


def draw_clouds(key, part):
    base_key = jax.random.fold_in(key, 21)
    where_key = jax.random.fold_in(key, 22)
    sign_key = jax.random.fold_in(key, 23)
    base = jnp.clip(jax.random.normal(base_key, (MEMB, M, DIM), jnp.float32), -6.0, 6.0)
    far_row = jax.random.randint(where_key, (MEMB,), 0, M)
    far_sign = (2 * jax.random.randint(sign_key, (MEMB,), 0, 2) - 1).astype(jnp.float32)
    row_index = jnp.arange(M, dtype=jnp.int32)
    is_far = row_index[None, :] == far_row[:, None]
    values = jnp.where(is_far[:, :, None], 6.0 * far_sign[:, None, None], base)
    return values.astype(jnp.bfloat16)


def setup_inputs(seed: int = 0, part: int = 0) -> dict:
    keys = jax.random.split(jax.random.key(seed), 4)
    part_splits = jax.random.split(jax.random.fold_in(keys[3], part), 4)
    return {
        "support": draw_support(jax.random.fold_in(jax.random.fold_in(keys[3], part), 71), part),
        "clouds": draw_clouds(jax.random.fold_in(jax.random.fold_in(keys[3], part), 71), part),
        "member_weights": jnp.clip(jnp.exp(jax.random.uniform(part_splits[2], (MEMB,), jnp.float32, math.log(1.0), math.log(10.0))), 1.0, 10.0),
    }


EPS = 0.05


def tile_cost(points, others):
    cross = lax.dot_general(points, others, (((1,), (1,)), ((), ())), preferred_element_type=jnp.float32)
    wide_a = points.astype(jnp.float32)
    wide_b = others.astype(jnp.float32)
    sq_a = jnp.sum(wide_a * wide_a, axis=1)
    sq_b = jnp.sum(wide_b * wide_b, axis=1)
    return (sq_a[:, None] + sq_b[None, :] - 2.0 * cross) / (2.0 * points.shape[1])


def reference(support, clouds, member_weights):
    count_n = support.shape[0]
    count_m = clouds.shape[1]
    log_n = jnp.log(jnp.float32(count_n))
    log_m = jnp.log(jnp.float32(count_m))
    weights = member_weights / jnp.sum(member_weights)

    def one_member(packed):
        cloud, weight = packed
        cost = tile_cost(support, cloud)
        pot_g = jnp.zeros((count_m,), jnp.float32)
        pot_f = jnp.zeros((count_n,), jnp.float32)
        for step in range(ITERS):
            pot_f = -EPS * jax.nn.logsumexp((pot_g[None, :] - cost) / EPS, axis=1) - EPS * log_n
            pot_g = -EPS * jax.nn.logsumexp((pot_f[:, None] - cost) / EPS, axis=0) - EPS * log_m
        plan = jnp.exp((pot_f[:, None] + pot_g[None, :] - cost) / EPS + log_n).astype(jnp.bfloat16)
        return weight * jnp.dot(plan, cloud, preferred_element_type=jnp.float32)

    terms = lax.map(one_member, (clouds, weights))
    return jnp.sum(terms, axis=0)
```

```python
import functools
import math

import jax
import jax.numpy as jnp
from jax import lax
from jax.experimental import pallas as pl
from jax.experimental.pallas import tpu as pltpu
from jax.sharding import PartitionSpec as P

ITERS = 3
EPS = 0.05
LANES = 128
GROUP = 32
EXTRA = 16
F32 = jnp.float32
BF16 = jnp.bfloat16


def split3(x):
    hi = x.astype(BF16).astype(F32)
    mid = (x - hi).astype(BF16).astype(F32)
    return hi, mid, (x - hi - mid).astype(BF16).astype(F32)


def kernel(
    dims, sup_ref, clouds_ref, weights_ref, out_ref,
    sup_send, cloud_send, sup_buf, cloud_buf, left, right, mat, top, u_ref, part,
    col, stat_send, stat_recv, plan, out_send, out_recv,
    sup_ssem, sup_rsem, cl_ssem, cl_rsem, relay_ssem, relay_rsem,
    stat_ssem, stat_rsem, out_ssem, out_rsem,
):
    memb, sib, shard, dim = dims
    devices = memb * sib
    rows = memb * shard
    cols = devices * shard
    chunk = 2048 if cols % 2048 == 0 else cols
    alpha = math.log2(math.e) / (EPS * 2.0 * dim)
    me = lax.axis_index("pts")
    mine = me // sib
    r = lax.rem(me, sib)

    def peer(d):
        return lax.rem(mine + d, memb)

    def at(cloud, place):
        return {"pts": cloud * sib + place}

    barrier = pltpu.get_barrier_semaphore()
    for d in range(1, memb):
        pl.semaphore_signal(barrier, inc=1, device_id=at(peer(d), r))
    for s in range(1, sib):
        pl.semaphore_signal(barrier, inc=1, device_id=at(mine, lax.rem(r + s, sib)))

    sup_send[...] = jnp.transpose(sup_ref[...].astype(F32)).astype(BF16)
    for k in range(memb):
        cloud_send[k] = jnp.transpose(clouds_ref[k].astype(F32)).astype(BF16)
    sup_buf[mine] = sup_send[...]
    cloud_buf[me] = cloud_send[mine]
    pl.semaphore_wait(barrier, memb - 1 + sib - 1)

    def cloud_copy(d):
        target = peer(d)
        return pltpu.make_async_remote_copy(
            cloud_send.at[target], cloud_buf.at[me], cl_ssem.at[d], cl_rsem.at[d],
            device_id=at(target, r), device_id_type=pl.DeviceIdType.MESH)

    def sup_copy(d):
        return pltpu.make_async_remote_copy(
            sup_send, sup_buf.at[mine], sup_ssem.at[d], sup_rsem.at[d],
            device_id=at(peer(d), r), device_id_type=pl.DeviceIdType.MESH)

    def relay_copy(d, s):
        owner = lax.rem(mine + memb - d, memb) * sib + r
        return pltpu.make_async_remote_copy(
            cloud_buf.at[owner], cloud_buf.at[owner], relay_ssem.at[d, s], relay_rsem.at[d, s],
            device_id=at(mine, lax.rem(r + s, sib)), device_id_type=pl.DeviceIdType.MESH)

    order = [memb // 2]
    for d in range(1, memb):
        if d not in order:
            order.append(d)
    for d in order:
        cloud_copy(d).start()
    for d in order:
        sup_copy(d).start()
    for s in range(1, sib):
        relay_copy(0, s).start()
    for d in range(1, memb):
        cloud_copy(d).wait_recv()
        for s in range(1, sib):
            relay_copy(d, s).start()

    ones3 = jnp.ones((3, shard), F32)
    zeros = jnp.zeros((EXTRA - 6, shard), F32)

    def make_left(c, _):
        x = sup_buf[c].astype(F32)
        norm = split3(-jnp.sum(x * x, axis=0, keepdims=True))
        block = jnp.concatenate([2.0 * x, ones3, *norm, zeros], axis=0)
        left[pl.ds(pl.multiple_of(c * shard, shard), shard), :] = jnp.transpose(block).astype(BF16)
        return 0

    def make_right(q, _):
        x = cloud_buf[q].astype(F32)
        norm = split3(-jnp.sum(x * x, axis=0, keepdims=True))
        block = jnp.concatenate([x, *norm, ones3, zeros], axis=0)
        right[:, pl.ds(pl.multiple_of(q * shard, shard), shard)] = block.astype(BF16)
        return 0

    for d in range(1, memb):
        sup_copy(d).wait_recv()
    lax.fori_loop(0, memb, make_left, 0)
    for d in range(memb):
        for s in range(1, sib):
            relay_copy(d, s).wait_recv()
    lax.fori_loop(0, devices, make_right, 0)

    wide = 256
    def cost_step(j, _):
        span = pl.ds(pl.multiple_of(j * wide, wide), wide)
        w = right[:, span]
        for i in range(0, rows, 256):
            h = slice(i, i + 256)
            t = jnp.dot(left[h, :], w, preferred_element_type=F32)
            mat[h, span] = t
            top[h, :] = jnp.maximum(top[h, :], jnp.maximum(t[:, :LANES], t[:, LANES:]))
        return 0

    top[...] = jnp.full(top.shape, -3e38, F32)
    lax.fori_loop(0, cols // wide, cost_step, 0)
    top[...] = jnp.broadcast_to(jnp.max(top[...], axis=1, keepdims=True), top.shape)

    tiles = chunk // LANES
    groups = rows // GROUP

    def tile(g, base, c):
        return (
            pl.ds(pl.multiple_of(g * GROUP, GROUP), GROUP),
            pl.ds(pl.multiple_of(base + c * LANES, LANES), LANES),
        )

    def rows_of(ref, g):
        return ref[pl.ds(pl.multiple_of(g * GROUP, GROUP), GROUP), :]

    def fold(x, op):
        acc = x[0:8]
        for i in range(8, GROUP, 8):
            acc = op(acc, x[i:i + 8])
        return acc

    def lanes(ref, base, c):
        return ref[:, base + c * LANES:base + (c + 1) * LANES]

    for base in range(0, cols, chunk):
        def max_step(g, best, base=base):
            a = rows_of(top, g)
            return tuple(
                jnp.maximum(best[c], fold(mat[tile(g, base, c)] - a, jnp.maximum))
                for c in range(tiles))

        start = tuple(jnp.full((8, LANES), -3e38, F32) for _ in range(tiles))
        best = lax.fori_loop(0, groups, max_step, start)
        for c in range(tiles):
            b = jnp.max(best[c], axis=0, keepdims=True)
            stat_send[0, :, base + c * LANES:base + (c + 1) * LANES] = b
            col[0, :, base + c * LANES:base + (c + 1) * LANES] = jnp.broadcast_to(b, (8, LANES))
            col[1, :, base + c * LANES:base + (c + 1) * LANES] = jnp.broadcast_to(
                jnp.exp2(b * alpha), (8, LANES))

    def stat_copy(step, s):
        n = 2 if step == 0 else 1
        lo = 0 if step == 0 else 1 + step
        return pltpu.make_async_remote_copy(
            stat_send.at[pl.ds(lo, n)], stat_recv.at[s, pl.ds(lo, n)],
            stat_ssem.at[step, s], stat_rsem.at[step, s],
            device_id=at(mine, lax.rem(r + s, sib)), device_id_type=pl.DeviceIdType.MESH)

    def times(x, y):
        return x * jnp.concatenate([y] * (GROUP // 8), axis=0)

    for step in range(ITERS):
        for base in range(0, cols, chunk):
            def row_step(g, _, base=base):
                acc = jnp.zeros((GROUP, LANES), F32)
                a = rows_of(top, g)
                for c in range(tiles):
                    k = mat[tile(g, base, c)]
                    if step == 0:
                        b = jnp.concatenate([lanes(col.at[0], base, c)] * (GROUP // 8), axis=0)
                        k = jnp.exp2(((k - a) - b) * alpha)
                        mat[tile(g, base, c)] = k
                    acc = acc + times(k, lanes(col.at[1], base, c))
                if base > 0:
                    acc = acc + rows_of(part, g)
                part[pl.ds(pl.multiple_of(g * GROUP, GROUP), GROUP), :] = acc
                return 0

            lax.fori_loop(0, groups, row_step, 0)
        total = jnp.sum(part[...], axis=1, keepdims=True)
        u_ref[...] = jnp.broadcast_to(1.0 / (total * rows_all(dims)), u_ref.shape)
        for base in range(0, cols, chunk):
            def col_step(g, acc, base=base):
                u = rows_of(u_ref, g)
                return tuple(
                    acc[c] + fold(mat[tile(g, base, c)] * u, jnp.add) for c in range(tiles))

            start = tuple(jnp.zeros((8, LANES), F32) for _ in range(tiles))
            acc = lax.fori_loop(0, groups, col_step, start)
            for c in range(tiles):
                stat_send[1 + step, :, base + c * LANES:base + (c + 1) * LANES] = jnp.sum(
                    acc[c], axis=0, keepdims=True)
        for s in range(1, sib):
            stat_copy(step, s).start()
        for s in range(1, sib):
            stat_copy(step, s).wait_recv()
        high = stat_send[0]
        for s in range(1, sib):
            high = jnp.maximum(high, stat_recv[s, 0])
        local = jnp.exp2((stat_send[0] - high) * alpha)
        total = local * stat_send[1 + step]
        for s in range(1, sib):
            total = total + jnp.exp2((stat_recv[s, 0] - high) * alpha) * stat_recv[s, 1 + step]
        v = local / (total * float(cols))
        col[1] = jnp.broadcast_to(v, (8, cols))

    weight_sum = weights_ref[0]
    for k in range(1, memb):
        weight_sum = weight_sum + weights_ref[k]
    weight = weights_ref[mine] / weight_sum

    def out_copy(d):
        target = peer(d)
        return pltpu.make_async_remote_copy(
            out_send.at[target], out_recv.at[mine], out_ssem.at[d], out_rsem.at[d],
            device_id=at(target, r), device_id_type=pl.DeviceIdType.MESH)

    for d in order + [0]:
        block = peer(d)

        def plan_step(g, _):
            u = rows_of(u_ref, block * (shard // GROUP) + g) * rows_all(dims)
            for base in range(0, cols, chunk):
                for c in range(tiles):
                    p = times(mat[tile(block * (shard // GROUP) + g, base, c)] * u,
                              lanes(col.at[1], base, c))
                    plan[pl.ds(pl.multiple_of(g * GROUP, GROUP), GROUP),
                         base + c * LANES:base + (c + 1) * LANES] = p.astype(BF16)
            return 0

        lax.fori_loop(0, shard // GROUP, plan_step, 0)
        term = lax.dot_general(
            plan[...], right[:dim, :], (((1,), (1,)), ((), ())), preferred_element_type=F32)
        term = jnp.transpose(term * weight)
        if d == 0:
            out_recv[mine] = term
        else:
            out_send[block] = term
            out_copy(d).start()

    for d in range(1, memb):
        out_copy(d).wait_recv()
    total = out_recv[0]
    for k in range(1, memb):
        total = total + out_recv[k]
    out_ref[...] = jnp.transpose(total)

    for d in range(1, memb):
        cloud_copy(d).wait_send()
        sup_copy(d).wait_send()
        out_copy(d).wait_send()
    for s in range(1, sib):
        for d in range(memb):
            relay_copy(d, s).wait_send()
        for step in range(ITERS):
            stat_copy(step, s).wait_send()


def rows_all(dims):
    memb, sib, shard, _ = dims
    return float(memb * sib * shard)


def per_device(support, clouds, member_weights):
    devices = lax.axis_size("pts")
    memb, shard, dim = clouds.shape
    sib = devices // memb
    rows, cols = memb * shard, devices * shard
    dims = (memb, sib, shard, dim)
    vmem, dma = pltpu.VMEM, pltpu.SemaphoreType.DMA
    return pl.pallas_call(
        functools.partial(kernel, dims),
        out_shape=jax.ShapeDtypeStruct((shard, dim), F32),
        in_specs=[
            pl.BlockSpec(memory_space=pltpu.VMEM),
            pl.BlockSpec(memory_space=pltpu.VMEM),
            pl.BlockSpec(memory_space=pltpu.SMEM),
        ],
        out_specs=pl.BlockSpec(memory_space=pltpu.VMEM),
        scratch_shapes=[
            vmem((dim, shard), BF16),
            vmem((memb, dim, shard), BF16),
            vmem((memb, dim, shard), BF16),
            vmem((devices, dim, shard), BF16),
            vmem((rows, dim + EXTRA), BF16),
            vmem((dim + EXTRA, cols), BF16),
            vmem((rows, cols), F32),
            vmem((rows, LANES), F32),
            vmem((rows, LANES), F32),
            vmem((rows, LANES), F32),
            vmem((2, 8, cols), F32),
            vmem((1 + ITERS, 1, cols), F32),
            vmem((sib, 1 + ITERS, 1, cols), F32),
            vmem((shard, cols), BF16),
            vmem((memb, dim, shard), F32),
            vmem((memb, dim, shard), F32),
            dma((memb,)), dma((memb,)),
            dma((memb,)), dma((memb,)),
            dma((memb, sib)), dma((memb, sib)),
            dma((ITERS, sib)), dma((ITERS, sib)),
            dma((memb,)), dma((memb,)),
        ],
        compiler_params=pltpu.CompilerParams(
            collective_id=0, has_side_effects=True,
            vmem_limit_bytes=rows * cols * 4 + (16 << 20)),
    )(support, clouds, member_weights)


def solution(mesh):
    in_specs = (P(("grp", "pts"), None), P(None, ("grp", "pts"), None), P("grp"))
    out_specs = P(("grp", "pts"), None)
    return jax.shard_map(
        per_device, mesh=mesh, in_specs=in_specs, out_specs=out_specs, check_vma=False
    )
```

```python
import functools
import math

import jax
import jax.numpy as jnp
from jax import lax
from jax.experimental import pallas as pl
from jax.experimental.pallas import tpu as pltpu
from jax.sharding import PartitionSpec as P

ITERS = 3
EPS = 0.05
LANES = 128
GROUP = 32
EXTRA = 16
F32 = jnp.float32
BF16 = jnp.bfloat16


def split3(x):
    hi = x.astype(BF16).astype(F32)
    mid = (x - hi).astype(BF16).astype(F32)
    return hi, mid, (x - hi - mid).astype(BF16).astype(F32)


def kernel(
    dims, sup_ref, clouds_ref, weights_ref, out_ref,
    sup_buf, cloud_buf, left, right, mat, top, u_ref, part,
    col, stat_send, stat_recv, plan, out_send, pair_recv, out_recv,
    sup_ssem, sup_rsem, pass_ssem, pass_rsem, cl_ssem, cl_rsem, relay_ssem, relay_rsem,
    stat_ssem, stat_rsem, pair_ssem, pair_rsem, out_ssem, out_rsem, own_sem,
):
    memb, sib, shard, dim = dims
    devices = memb * sib
    rows = memb * shard
    cols = devices * shard
    chunk = 2048 if cols % 2048 == 0 else cols
    alpha = math.log2(math.e) / (EPS * 2.0 * dim)
    me = lax.axis_index("pts")
    mine = me // sib
    r = lax.rem(me, sib)
    outer = memb // 2
    line, side = mine // 2, lax.rem(mine, 2)
    twin = line * 2 + 1 - side

    def peer(d):
        return lax.rem(mine + d, memb)

    def at(cloud, place):
        return {"pts": cloud * sib + place}

    barrier = pltpu.get_barrier_semaphore()
    for d in range(1, memb):
        pl.semaphore_signal(barrier, inc=1, device_id=at(peer(d), r))
    for s in range(1, sib):
        pl.semaphore_signal(barrier, inc=1, device_id=at(mine, lax.rem(r + s, sib)))

    own_sup = pltpu.make_async_copy(sup_ref, sup_buf.at[mine], own_sem.at[0])
    own_cloud = pltpu.make_async_copy(clouds_ref.at[mine], cloud_buf.at[me], own_sem.at[1])
    own_sup.start()
    own_cloud.start()
    pl.semaphore_wait(barrier, memb - 1 + sib - 1)

    def cloud_copy(d):
        target = peer(d)
        return pltpu.make_async_remote_copy(
            clouds_ref.at[target], cloud_buf.at[me], cl_ssem.at[d], cl_rsem.at[d],
            device_id=at(target, r), device_id_type=pl.DeviceIdType.MESH)

    def sup_copy(e):
        target = lax.rem(line + e, outer) * 2 + side
        return pltpu.make_async_remote_copy(
            sup_ref, sup_buf.at[mine], sup_ssem.at[e], sup_rsem.at[e],
            device_id=at(target, r), device_id_type=pl.DeviceIdType.MESH)

    def pass_copy(e):
        owner = lax.rem(line + outer - e, outer) * 2 + side
        return pltpu.make_async_remote_copy(
            sup_buf.at[owner], sup_buf.at[owner], pass_ssem.at[e], pass_rsem.at[e],
            device_id=at(twin, r), device_id_type=pl.DeviceIdType.MESH)

    def relay_copy(d, s):
        owner = lax.rem(mine + memb - d, memb) * sib + r
        return pltpu.make_async_remote_copy(
            cloud_buf.at[owner], cloud_buf.at[owner], relay_ssem.at[d, s], relay_rsem.at[d, s],
            device_id=at(mine, lax.rem(r + s, sib)), device_id_type=pl.DeviceIdType.MESH)

    def dist(i):
        j = lax.rem(i + memb - 1, memb) + 1
        return memb // 2 + (j // 2) * (2 * lax.rem(j, 2) - 1)

    for e in range(1, outer):
        sup_copy(e).start()

    def send_step(i, _):
        cloud_copy(dist(i)).start()
        return 0

    lax.fori_loop(1, memb, send_step, 0)
    own_sup.wait()
    pass_copy(0).start()
    own_cloud.wait()
    for s in range(1, sib):
        relay_copy(0, s).start()
    for e in range(1, outer):
        sup_copy(e).wait_recv()
        pass_copy(e).start()
    for e in range(outer):
        pass_copy(e).wait_recv()

    ones3 = jnp.ones((3, shard), F32)
    zeros = jnp.zeros((EXTRA - 6, shard), F32)

    def make_left(c, _):
        x = sup_buf[c].astype(F32)
        norm = split3(-jnp.sum(x * x, axis=0, keepdims=True))
        block = jnp.concatenate([2.0 * x, ones3, *norm, zeros], axis=0)
        left[pl.ds(pl.multiple_of(c * shard, shard), shard), :] = jnp.transpose(block).astype(BF16)
        return 0

    def make_right(q, _):
        x = cloud_buf[q].astype(F32)
        norm = split3(-jnp.sum(x * x, axis=0, keepdims=True))
        block = jnp.concatenate([x, *norm, ones3, zeros], axis=0)
        right[:, pl.ds(pl.multiple_of(q * shard, shard), shard)] = block.astype(BF16)
        return 0

    lax.fori_loop(0, memb, make_left, 0)

    block_cols = sib * shard
    wide = 256 if block_cols % 256 == 0 else LANES
    top[...] = jnp.full(top.shape, -3e38, F32)

    def arrive_step(i, _):
        @pl.when(i < memb - 1)
        def _():
            cloud_copy(dist(i + 1)).wait_recv()
            for s in range(1, sib):
                relay_copy(dist(i + 1), s).start()

        d = dist(i)
        for s in range(1, sib):
            relay_copy(d, s).wait_recv()
        owner = lax.rem(mine + memb - d, memb)
        lax.fori_loop(0, sib, lambda q, _: make_right(owner * sib + q, 0), 0)

        def cost_step(j, _):
            span = pl.ds(pl.multiple_of(owner * block_cols + j * wide, wide), wide)
            w = right[:, span]
            for h in range(0, rows, 256):
                t = jnp.dot(left[h:h + 256, :], w, preferred_element_type=F32)
                mat[h:h + 256, span] = t
                most = t[:, :LANES]
                for n in range(LANES, wide, LANES):
                    most = jnp.maximum(most, t[:, n:n + LANES])
                top[h:h + 256, :] = jnp.maximum(top[h:h + 256, :], most)
            return 0

        lax.fori_loop(0, block_cols // wide, cost_step, 0)
        return 0

    lax.fori_loop(0, memb, arrive_step, 0)
    top[...] = jnp.broadcast_to(jnp.max(top[...], axis=1, keepdims=True), top.shape)

    tiles = chunk // LANES
    groups = rows // GROUP

    def tile(g, base, c):
        return (
            pl.ds(pl.multiple_of(g * GROUP, GROUP), GROUP),
            pl.ds(pl.multiple_of(base + c * LANES, LANES), LANES),
        )

    def rows_of(ref, g):
        return ref[pl.ds(pl.multiple_of(g * GROUP, GROUP), GROUP), :]

    def fold(x, op):
        acc = x[0:8]
        for i in range(8, GROUP, 8):
            acc = op(acc, x[i:i + 8])
        return acc

    def lanes(ref, base, c):
        return ref[:, base + c * LANES:base + (c + 1) * LANES]

    for base in range(0, cols, chunk):
        def max_step(g, best, base=base):
            a = rows_of(top, g)
            return tuple(
                jnp.maximum(best[c], fold(mat[tile(g, base, c)] - a, jnp.maximum))
                for c in range(tiles))

        start = tuple(jnp.full((8, LANES), -3e38, F32) for _ in range(tiles))
        best = lax.fori_loop(0, groups, max_step, start)
        for c in range(tiles):
            b = jnp.max(best[c], axis=0, keepdims=True)
            stat_send[0, :, base + c * LANES:base + (c + 1) * LANES] = b
            col[0, :, base + c * LANES:base + (c + 1) * LANES] = jnp.broadcast_to(b, (8, LANES))
            col[1, :, base + c * LANES:base + (c + 1) * LANES] = jnp.broadcast_to(
                jnp.exp2(b * alpha), (8, LANES))

    def stat_copy(step, s):
        n = 2 if step == 0 else 1
        lo = 0 if step == 0 else 1 + step
        return pltpu.make_async_remote_copy(
            stat_send.at[pl.ds(lo, n)], stat_recv.at[s, pl.ds(lo, n)],
            stat_ssem.at[step, s], stat_rsem.at[step, s],
            device_id=at(mine, lax.rem(r + s, sib)), device_id_type=pl.DeviceIdType.MESH)

    def times(x, y):
        return x * jnp.concatenate([y] * (GROUP // 8), axis=0)

    for step in range(ITERS):
        for base in range(0, cols, chunk):
            def row_step(g, _, base=base):
                acc = jnp.zeros((GROUP, LANES), F32)
                a = rows_of(top, g)
                for c in range(tiles):
                    k = mat[tile(g, base, c)]
                    if step == 0:
                        b = jnp.concatenate([lanes(col.at[0], base, c)] * (GROUP // 8), axis=0)
                        k = jnp.exp2(((k - a) - b) * alpha)
                        mat[tile(g, base, c)] = k
                    acc = acc + times(k, lanes(col.at[1], base, c))
                if base > 0:
                    acc = acc + rows_of(part, g)
                part[pl.ds(pl.multiple_of(g * GROUP, GROUP), GROUP), :] = acc
                return 0

            lax.fori_loop(0, groups, row_step, 0)
        total = jnp.sum(part[...], axis=1, keepdims=True)
        u_ref[...] = jnp.broadcast_to(1.0 / (total * rows_all(dims)), u_ref.shape)
        for base in range(0, cols, chunk):
            def col_step(g, acc, base=base):
                u = rows_of(u_ref, g)
                return tuple(
                    acc[c] + fold(mat[tile(g, base, c)] * u, jnp.add) for c in range(tiles))

            start = tuple(jnp.zeros((8, LANES), F32) for _ in range(tiles))
            acc = lax.fori_loop(0, groups, col_step, start)
            for c in range(tiles):
                stat_send[1 + step, :, base + c * LANES:base + (c + 1) * LANES] = jnp.sum(
                    acc[c], axis=0, keepdims=True)
        for s in range(1, sib):
            stat_copy(step, s).start()
        for s in range(1, sib):
            stat_copy(step, s).wait_recv()
        high = stat_send[0]
        for s in range(1, sib):
            high = jnp.maximum(high, stat_recv[s, 0])
        local = jnp.exp2((stat_send[0] - high) * alpha)
        total = local * stat_send[1 + step]
        for s in range(1, sib):
            total = total + jnp.exp2((stat_recv[s, 0] - high) * alpha) * stat_recv[s, 1 + step]
        v = local / (total * float(cols))
        col[1] = jnp.broadcast_to(v, (8, cols))

    weight_sum = weights_ref[0]
    for k in range(1, memb):
        weight_sum = weight_sum + weights_ref[k]
    weight = weights_ref[mine] / weight_sum

    def pair_copy(e):
        target = lax.rem(line + e, outer)
        return pltpu.make_async_remote_copy(
            out_send.at[target * 2 + 1 - side], pair_recv.at[target],
            pair_ssem.at[e], pair_rsem.at[e],
            device_id=at(twin, r), device_id_type=pl.DeviceIdType.MESH)

    def out_copy(e):
        target = lax.rem(line + e, outer) * 2 + side
        return pltpu.make_async_remote_copy(
            out_send.at[target], out_recv.at[e], out_ssem.at[e], out_rsem.at[e],
            device_id=at(target, r), device_id_type=pl.DeviceIdType.MESH)

    def send_block(i, _):
        second = i // outer
        e = outer - 1 - lax.rem(i, outer)
        target = lax.rem(line + e, outer)
        block = target * 2 + lax.rem(side + 1 + second, 2)

        def plan_step(g, _):
            u = rows_of(u_ref, block * (shard // GROUP) + g) * rows_all(dims)
            for base in range(0, cols, chunk):
                for c in range(tiles):
                    p = times(mat[tile(block * (shard // GROUP) + g, base, c)] * u,
                              lanes(col.at[1], base, c))
                    plan[pl.ds(pl.multiple_of(g * GROUP, GROUP), GROUP),
                         base + c * LANES:base + (c + 1) * LANES] = p.astype(BF16)
            return 0

        lax.fori_loop(0, shard // GROUP, plan_step, 0)
        term = lax.dot_general(
            plan[...], right[:dim, :], (((1,), (1,)), ((), ())), preferred_element_type=F32)
        term = jnp.transpose(term * weight)

        @pl.when(second == 0)
        def _():
            out_send[block] = term
            pair_copy(e).start()

        @pl.when(second == 1)
        def _():
            pair_copy(e).wait_recv()
            out_send[block] = term + pair_recv[target]

            @pl.when(e > 0)
            def _():
                out_copy(e).start()

        return 0

    lax.fori_loop(0, memb, send_block, 0)
    total = out_send[mine]
    for e in range(1, outer):
        out_copy(e).wait_recv()
        total = total + out_recv[e]
    out_ref[...] = total

    for d in range(1, memb):
        cloud_copy(d).wait_send()
    for e in range(outer):
        pass_copy(e).wait_send()
        pair_copy(e).wait_send()
        if e > 0:
            sup_copy(e).wait_send()
            out_copy(e).wait_send()
    for s in range(1, sib):
        for d in range(memb):
            relay_copy(d, s).wait_send()
        for step in range(ITERS):
            stat_copy(step, s).wait_send()


def rows_all(dims):
    memb, sib, shard, _ = dims
    return float(memb * sib * shard)


def per_device(support, clouds, member_weights):
    devices = lax.axis_size("pts")
    memb, shard, dim = clouds.shape
    sib = devices // memb
    rows, cols = memb * shard, devices * shard
    dims = (memb, sib, shard, dim)
    vmem, dma = pltpu.VMEM, pltpu.SemaphoreType.DMA
    out = pl.pallas_call(
        functools.partial(kernel, dims),
        out_shape=jax.ShapeDtypeStruct((dim, shard), F32),
        in_specs=[
            pl.BlockSpec(memory_space=pl.ANY),
            pl.BlockSpec(memory_space=pl.ANY),
            pl.BlockSpec(memory_space=pltpu.SMEM),
        ],
        out_specs=pl.BlockSpec(memory_space=pltpu.VMEM),
        scratch_shapes=[
            vmem((memb, dim, shard), BF16),
            vmem((devices, dim, shard), BF16),
            vmem((rows, dim + EXTRA), BF16),
            vmem((dim + EXTRA, cols), BF16),
            vmem((rows, cols), F32),
            vmem((rows, LANES), F32),
            vmem((rows, LANES), F32),
            vmem((rows, LANES), F32),
            vmem((2, 8, cols), F32),
            vmem((1 + ITERS, 1, cols), F32),
            vmem((sib, 1 + ITERS, 1, cols), F32),
            vmem((shard, cols), BF16),
            vmem((memb, dim, shard), F32),
            vmem((memb // 2, dim, shard), F32),
            vmem((memb // 2, dim, shard), F32),
            dma((memb // 2,)), dma((memb // 2,)),
            dma((memb // 2,)), dma((memb // 2,)),
            dma((memb,)), dma((memb,)),
            dma((memb, sib)), dma((memb, sib)),
            dma((ITERS, sib)), dma((ITERS, sib)),
            dma((memb // 2,)), dma((memb // 2,)),
            dma((memb // 2,)), dma((memb // 2,)), dma((2,)),
        ],
        compiler_params=pltpu.CompilerParams(
            collective_id=0, has_side_effects=True,
            vmem_limit_bytes=rows * cols * 4 + (16 << 20)),
    )(support.T, clouds.swapaxes(1, 2), member_weights)
    return out.T


def solution(mesh):
    in_specs = (P(("grp", "pts"), None), P(None, ("grp", "pts"), None), P("grp"))
    out_specs = P(("grp", "pts"), None)
    return jax.shard_map(
        per_device, mesh=mesh, in_specs=in_specs, out_specs=out_specs, check_vma=False
    )
```

```python
import functools
import math

import jax
import jax.numpy as jnp
from jax import lax
from jax.experimental import pallas as pl
from jax.experimental.pallas import tpu as pltpu
from jax.sharding import PartitionSpec as P

ITERS = 3
EPS = 0.05
LANES = 128
GROUP = 64
EXTRA = 16
F32 = jnp.float32
BF16 = jnp.bfloat16


def split3(x):
    hi = x.astype(BF16).astype(F32)
    mid = (x - hi).astype(BF16).astype(F32)
    return hi, mid, (x - hi - mid).astype(BF16).astype(F32)


def kernel(
    dims, sup_ref, clouds_ref, weights_ref, out_ref,
    cloud_send, sup_buf, cloud_buf, left, right, mat, top, u_ref, part,
    col, stat_send, stat_recv, plan, out_send, out_recv,
    sup_ssem, sup_rsem, cl_ssem, cl_rsem, relay_ssem, relay_rsem,
    stat_ssem, stat_rsem, out_ssem, out_rsem, own_sem,
):
    memb, sib, shard, dim = dims
    devices = memb * sib
    rows = memb * shard
    cols = devices * shard
    chunk = 2048 if cols % 2048 == 0 else cols
    alpha = math.log2(math.e) / (EPS * 2.0 * dim)
    me = lax.axis_index("pts")
    mine = me // sib
    r = lax.rem(me, sib)

    def peer(d):
        return lax.rem(mine + d, memb)

    def at(cloud, place):
        return {"pts": cloud * sib + place}

    barrier = pltpu.get_barrier_semaphore()
    for d in range(1, memb):
        pl.semaphore_signal(barrier, inc=1, device_id=at(peer(d), r))
    for s in range(1, sib):
        pl.semaphore_signal(barrier, inc=1, device_id=at(mine, lax.rem(r + s, sib)))

    own_sup = pltpu.make_async_copy(sup_ref, sup_buf.at[mine], own_sem.at[0])
    own_cloud = pltpu.make_async_copy(clouds_ref.at[mine], cloud_buf.at[me], own_sem.at[1])
    staged = pltpu.make_async_copy(clouds_ref, cloud_send, own_sem.at[2])
    staged.start()
    own_sup.start()
    own_cloud.start()
    own_sup.wait()
    own_cloud.wait()
    staged.wait()
    pl.semaphore_wait(barrier, memb - 1 + sib - 1)

    def cloud_copy(d):
        target = peer(d)
        return pltpu.make_async_remote_copy(
            cloud_send.at[target], cloud_buf.at[me], cl_ssem.at[d], cl_rsem.at[d],
            device_id=at(target, r), device_id_type=pl.DeviceIdType.MESH)

    def sup_copy(d):
        return pltpu.make_async_remote_copy(
            sup_buf.at[mine], sup_buf.at[mine], sup_ssem.at[d], sup_rsem.at[d],
            device_id=at(peer(d), r), device_id_type=pl.DeviceIdType.MESH)

    def relay_copy(d, s):
        owner = lax.rem(mine + memb - d, memb) * sib + r
        return pltpu.make_async_remote_copy(
            cloud_buf.at[owner], cloud_buf.at[owner], relay_ssem.at[d, s], relay_rsem.at[d, s],
            device_id=at(mine, lax.rem(r + s, sib)), device_id_type=pl.DeviceIdType.MESH)

    order = [memb // 2]
    for d in range(1, memb):
        if d not in order:
            order.append(d)
    for d in order:
        sup_copy(d).start()
    for d in order:
        cloud_copy(d).start()
    for s in range(1, sib):
        relay_copy(0, s).start()

    ones3 = jnp.ones((3, shard), F32)
    zeros = jnp.zeros((EXTRA - 6, shard), F32)

    def make_left(c, _):
        x = sup_buf[c].astype(F32)
        norm = split3(-jnp.sum(x * x, axis=0, keepdims=True))
        block = jnp.concatenate([2.0 * x, ones3, *norm, zeros], axis=0)
        left[pl.ds(pl.multiple_of(c * shard, shard), shard), :] = jnp.transpose(block).astype(BF16)
        return 0

    def make_right(q, _):
        x = cloud_buf[q].astype(F32)
        norm = split3(-jnp.sum(x * x, axis=0, keepdims=True))
        block = jnp.concatenate([x, *norm, ones3, zeros], axis=0)
        right[:, pl.ds(pl.multiple_of(q * shard, shard), shard)] = block.astype(BF16)
        return 0

    for d in range(1, memb):
        sup_copy(d).wait_recv()
    lax.fori_loop(0, memb, make_left, 0, unroll=2)
    for d in range(1, memb):
        cloud_copy(d).wait_recv()
        for s in range(1, sib):
            relay_copy(d, s).start()
    for d in range(memb):
        for s in range(1, sib):
            relay_copy(d, s).wait_recv()
    lax.fori_loop(0, devices, make_right, 0, unroll=4)

    wide = 256
    def cost_step(j, _):
        span = pl.ds(pl.multiple_of(j * wide, wide), wide)
        w = right[:, span]
        for i in range(0, rows, 256):
            h = slice(i, i + 256)
            t = jnp.dot(left[h, :], w, preferred_element_type=F32)
            mat[h, span] = t
            top[h, :] = jnp.maximum(top[h, :], jnp.maximum(t[:, :LANES], t[:, LANES:]))
        return 0

    top[...] = jnp.full(top.shape, -3e38, F32)
    lax.fori_loop(0, cols // wide, cost_step, 0)
    top[...] = jnp.broadcast_to(jnp.max(top[...], axis=1, keepdims=True), top.shape)

    tiles = chunk // LANES
    groups = rows // GROUP

    def tile(g, base, c):
        return (
            pl.ds(pl.multiple_of(g * GROUP, GROUP), GROUP),
            pl.ds(pl.multiple_of(base + c * LANES, LANES), LANES),
        )

    def rows_of(ref, g):
        return ref[pl.ds(pl.multiple_of(g * GROUP, GROUP), GROUP), :]

    def fold(x, op):
        acc = x[0:8]
        for i in range(8, GROUP, 8):
            acc = op(acc, x[i:i + 8])
        return acc

    def lanes(ref, base, c):
        return ref[:, base + c * LANES:base + (c + 1) * LANES]

    for base in range(0, cols, chunk):
        def max_step(g, best, base=base):
            a = rows_of(top, g)
            return tuple(
                jnp.maximum(best[c], fold(mat[tile(g, base, c)] - a, jnp.maximum))
                for c in range(tiles))

        start = tuple(jnp.full((8, LANES), -3e38, F32) for _ in range(tiles))
        best = lax.fori_loop(0, groups, max_step, start, unroll=2)
        for c in range(tiles):
            b = jnp.max(best[c], axis=0, keepdims=True)
            stat_send[0, :, base + c * LANES:base + (c + 1) * LANES] = b
            col[0, :, base + c * LANES:base + (c + 1) * LANES] = jnp.broadcast_to(b, (8, LANES))
            col[1, :, base + c * LANES:base + (c + 1) * LANES] = jnp.broadcast_to(
                jnp.exp2(b * alpha), (8, LANES))

    def stat_copy(step, s):
        n = 2 if step == 0 else 1
        lo = 0 if step == 0 else 1 + step
        return pltpu.make_async_remote_copy(
            stat_send.at[pl.ds(lo, n)], stat_recv.at[s, pl.ds(lo, n)],
            stat_ssem.at[step, s], stat_rsem.at[step, s],
            device_id=at(mine, lax.rem(r + s, sib)), device_id_type=pl.DeviceIdType.MESH)

    def times(x, y):
        return x * jnp.concatenate([y] * (GROUP // 8), axis=0)

    for step in range(ITERS):
        for base in range(0, cols, chunk):
            def row_step(g, _, base=base):
                acc = jnp.zeros((GROUP, LANES), F32)
                a = rows_of(top, g)
                for c in range(tiles):
                    k = mat[tile(g, base, c)]
                    if step == 0:
                        b = jnp.concatenate([lanes(col.at[0], base, c)] * (GROUP // 8), axis=0)
                        k = jnp.exp2(((k - a) - b) * alpha)
                        mat[tile(g, base, c)] = k
                    acc = acc + times(k, lanes(col.at[1], base, c))
                if base > 0:
                    acc = acc + rows_of(part, g)
                part[pl.ds(pl.multiple_of(g * GROUP, GROUP), GROUP), :] = acc
                return 0

            lax.fori_loop(0, groups, row_step, 0, unroll=2)
        total = jnp.sum(part[...], axis=1, keepdims=True)
        u_ref[...] = jnp.broadcast_to(1.0 / (total * rows_all(dims)), u_ref.shape)
        for base in range(0, cols, chunk):
            def col_step(g, acc, base=base):
                u = rows_of(u_ref, g)
                return tuple(
                    acc[c] + fold(mat[tile(g, base, c)] * u, jnp.add) for c in range(tiles))

            start = tuple(jnp.zeros((8, LANES), F32) for _ in range(tiles))
            acc = lax.fori_loop(0, groups, col_step, start, unroll=2)
            for c in range(tiles):
                stat_send[1 + step, :, base + c * LANES:base + (c + 1) * LANES] = jnp.sum(
                    acc[c], axis=0, keepdims=True)
        for s in range(1, sib):
            stat_copy(step, s).start()
        for s in range(1, sib):
            stat_copy(step, s).wait_recv()
        high = stat_send[0]
        for s in range(1, sib):
            high = jnp.maximum(high, stat_recv[s, 0])
        local = jnp.exp2((stat_send[0] - high) * alpha)
        total = local * stat_send[1 + step]
        for s in range(1, sib):
            total = total + jnp.exp2((stat_recv[s, 0] - high) * alpha) * stat_recv[s, 1 + step]
        v = local / (total * float(cols))
        col[1] = jnp.broadcast_to(v, (8, cols))

    weight_sum = weights_ref[0]
    for k in range(1, memb):
        weight_sum = weight_sum + weights_ref[k]
    weight = weights_ref[mine] / weight_sum

    def out_copy(d):
        target = peer(d)
        return pltpu.make_async_remote_copy(
            out_send.at[target], out_recv.at[mine], out_ssem.at[d], out_rsem.at[d],
            device_id=at(target, r), device_id_type=pl.DeviceIdType.MESH)

    for d in order + [0]:
        block = peer(d)

        def plan_step(g, _):
            u = rows_of(u_ref, block * (shard // GROUP) + g) * rows_all(dims)
            for base in range(0, cols, chunk):
                for c in range(tiles):
                    p = times(mat[tile(block * (shard // GROUP) + g, base, c)] * u,
                              lanes(col.at[1], base, c))
                    plan[pl.ds(pl.multiple_of(g * GROUP, GROUP), GROUP),
                         base + c * LANES:base + (c + 1) * LANES] = p.astype(BF16)
            return 0

        lax.fori_loop(0, shard // GROUP, plan_step, 0)
        term = lax.dot_general(
            plan[...], right[:dim, :], (((1,), (1,)), ((), ())), preferred_element_type=F32)
        term = jnp.transpose(term * weight)
        if d == 0:
            out_recv[mine] = term
        else:
            out_send[block] = term
            out_copy(d).start()

    for d in range(1, memb):
        out_copy(d).wait_recv()
    total = out_recv[0]
    for k in range(1, memb):
        total = total + out_recv[k]
    out_ref[...] = total

    for d in range(1, memb):
        cloud_copy(d).wait_send()
        sup_copy(d).wait_send()
        out_copy(d).wait_send()
    for s in range(1, sib):
        for d in range(memb):
            relay_copy(d, s).wait_send()
        for step in range(ITERS):
            stat_copy(step, s).wait_send()


def rows_all(dims):
    memb, sib, shard, _ = dims
    return float(memb * sib * shard)


def per_device(support, clouds, member_weights):
    devices = lax.axis_size("pts")
    memb, shard, dim = clouds.shape
    sib = devices // memb
    rows, cols = memb * shard, devices * shard
    dims = (memb, sib, shard, dim)
    vmem, dma = pltpu.VMEM, pltpu.SemaphoreType.DMA
    out = pl.pallas_call(
        functools.partial(kernel, dims),
        out_shape=jax.ShapeDtypeStruct((dim, shard), F32),
        in_specs=[
            pl.BlockSpec(memory_space=pl.ANY),
            pl.BlockSpec(memory_space=pl.ANY),
            pl.BlockSpec(memory_space=pltpu.SMEM),
        ],
        out_specs=pl.BlockSpec(memory_space=pltpu.VMEM),
        scratch_shapes=[
            vmem((memb, dim, shard), BF16),
            vmem((memb, dim, shard), BF16),
            vmem((devices, dim, shard), BF16),
            vmem((rows, dim + EXTRA), BF16),
            vmem((dim + EXTRA, cols), BF16),
            vmem((rows, cols), F32),
            vmem((rows, LANES), F32),
            vmem((rows, LANES), F32),
            vmem((rows, LANES), F32),
            vmem((2, 8, cols), F32),
            vmem((1 + ITERS, 1, cols), F32),
            vmem((sib, 1 + ITERS, 1, cols), F32),
            vmem((shard, cols), BF16),
            vmem((memb, dim, shard), F32),
            vmem((memb, dim, shard), F32),
            dma((memb,)), dma((memb,)),
            dma((memb,)), dma((memb,)),
            dma((memb, sib)), dma((memb, sib)),
            dma((ITERS, sib)), dma((ITERS, sib)),
            dma((memb,)), dma((memb,)), dma((3,)),
        ],
        compiler_params=pltpu.CompilerParams(
            collective_id=0, has_side_effects=True,
            vmem_limit_bytes=rows * cols * 4 + (16 << 20)),
    )(support.T, clouds.swapaxes(1, 2), member_weights)
    return out.T


def solution(mesh):
    in_specs = (P(("grp", "pts"), None), P(None, ("grp", "pts"), None), P("grp"))
    out_specs = P(("grp", "pts"), None)
    return jax.shard_map(
        per_device, mesh=mesh, in_specs=in_specs, out_specs=out_specs, check_vma=False
    )
```

```python
import functools
import math

import jax
import jax.numpy as jnp
from jax import lax
from jax.experimental import pallas as pl
from jax.experimental.pallas import tpu as pltpu
from jax.sharding import PartitionSpec as P

ITERS = 3
EPS = 0.05
LANES = 128
GROUP = 64
EXTRA = 16
F32 = jnp.float32
BF16 = jnp.bfloat16


def split3(x):
    hi = x.astype(BF16).astype(F32)
    mid = (x - hi).astype(BF16).astype(F32)
    return hi, mid, (x - hi - mid).astype(BF16).astype(F32)


def kernel(
    dims, sup_ref, clouds_ref, weights_ref, out_ref,
    cloud_send, sup_buf, cloud_buf, left, right, mat, top, u_ref, part,
    col, stat_send, stat_recv, plan, out_send, out_recv,
    sup_ssem, sup_rsem, cl_ssem, cl_rsem, relay_ssem, relay_rsem,
    stat_ssem, stat_rsem, out_ssem, out_rsem, own_sem,
):
    memb, sib, shard, dim = dims
    devices = memb * sib
    rows = memb * shard
    cols = devices * shard
    chunk = 2048 if cols % 2048 == 0 else cols
    alpha = math.log2(math.e) / (EPS * 2.0 * dim)
    me = lax.axis_index("pts")
    mine = me // sib
    r = lax.rem(me, sib)

    def peer(d):
        return lax.rem(mine + d, memb)

    def at(cloud, place):
        return {"pts": cloud * sib + place}

    barrier = pltpu.get_barrier_semaphore()
    for d in range(1, memb):
        pl.semaphore_signal(barrier, inc=1, device_id=at(peer(d), r))
    for s in range(1, sib):
        pl.semaphore_signal(barrier, inc=1, device_id=at(mine, lax.rem(r + s, sib)))

    own_sup = pltpu.make_async_copy(sup_ref, sup_buf.at[mine], own_sem.at[0])
    own_cloud = pltpu.make_async_copy(clouds_ref.at[mine], cloud_buf.at[me], own_sem.at[1])
    staged = pltpu.make_async_copy(clouds_ref, cloud_send, own_sem.at[2])
    staged.start()
    own_sup.start()
    own_cloud.start()
    own_sup.wait()
    own_cloud.wait()
    staged.wait()
    pl.semaphore_wait(barrier, memb - 1 + sib - 1)

    def cloud_copy(d):
        target = peer(d)
        return pltpu.make_async_remote_copy(
            cloud_send.at[target], cloud_buf.at[me], cl_ssem.at[d], cl_rsem.at[d],
            device_id=at(target, r), device_id_type=pl.DeviceIdType.MESH)

    def sup_copy(d):
        return pltpu.make_async_remote_copy(
            sup_buf.at[mine], sup_buf.at[mine], sup_ssem.at[d], sup_rsem.at[d],
            device_id=at(peer(d), r), device_id_type=pl.DeviceIdType.MESH)

    def relay_copy(d, s):
        owner = lax.rem(mine + memb - d, memb) * sib + r
        return pltpu.make_async_remote_copy(
            cloud_buf.at[owner], cloud_buf.at[owner], relay_ssem.at[d, s], relay_rsem.at[d, s],
            device_id=at(mine, lax.rem(r + s, sib)), device_id_type=pl.DeviceIdType.MESH)

    order = [memb // 2]
    for d in range(1, memb):
        if d not in order:
            order.append(d)
    for d in order:
        sup_copy(d).start()
    for d in order:
        cloud_copy(d).start()
    for s in range(1, sib):
        relay_copy(0, s).start()

    ones3 = jnp.ones((3, shard), F32)
    zeros = jnp.zeros((EXTRA - 6, shard), F32)

    def make_left(c, _):
        x = sup_buf[c].astype(F32)
        norm = split3(-jnp.sum(x * x, axis=0, keepdims=True))
        block = jnp.concatenate([2.0 * x, ones3, *norm, zeros], axis=0)
        left[pl.ds(pl.multiple_of(c * shard, shard), shard), :] = jnp.transpose(block).astype(BF16)
        return 0

    def make_right(q, _):
        x = cloud_buf[q].astype(F32)
        norm = split3(-jnp.sum(x * x, axis=0, keepdims=True))
        block = jnp.concatenate([x, *norm, ones3, zeros], axis=0)
        right[:, pl.ds(pl.multiple_of(q * shard, shard), shard)] = block.astype(BF16)
        return 0

    for d in range(1, memb):
        sup_copy(d).wait_recv()
    lax.fori_loop(0, memb, make_left, 0, unroll=4)
    for d in range(1, memb):
        cloud_copy(d).wait_recv()
        for s in range(1, sib):
            relay_copy(d, s).start()
    for d in range(memb):
        for s in range(1, sib):
            relay_copy(d, s).wait_recv()
    lax.fori_loop(0, devices, make_right, 0, unroll=4)

    wide = 256
    def cost_step(j, _):
        span = pl.ds(pl.multiple_of(j * wide, wide), wide)
        w = right[:, span]
        for i in range(0, rows, 256):
            h = slice(i, i + 256)
            t = jnp.dot(left[h, :], w, preferred_element_type=F32)
            mat[h, span] = t
            top[h, :] = jnp.maximum(top[h, :], jnp.maximum(t[:, :LANES], t[:, LANES:]))
        return 0

    top[...] = jnp.full(top.shape, -3e38, F32)
    lax.fori_loop(0, cols // wide, cost_step, 0, unroll=2)
    top[...] = jnp.broadcast_to(jnp.max(top[...], axis=1, keepdims=True), top.shape)

    tiles = chunk // LANES
    groups = rows // GROUP

    def tile(g, base, c):
        return (
            pl.ds(pl.multiple_of(g * GROUP, GROUP), GROUP),
            pl.ds(pl.multiple_of(base + c * LANES, LANES), LANES),
        )

    def rows_of(ref, g):
        return ref[pl.ds(pl.multiple_of(g * GROUP, GROUP), GROUP), :]

    def fold(x, op):
        acc = x[0:8]
        for i in range(8, GROUP, 8):
            acc = op(acc, x[i:i + 8])
        return acc

    def lanes(ref, base, c):
        return ref[:, base + c * LANES:base + (c + 1) * LANES]

    for base in range(0, cols, chunk):
        def max_step(g, best, base=base):
            a = rows_of(top, g)
            return tuple(
                jnp.maximum(best[c], fold(mat[tile(g, base, c)] - a, jnp.maximum))
                for c in range(tiles))

        start = tuple(jnp.full((8, LANES), -3e38, F32) for _ in range(tiles))
        best = lax.fori_loop(0, groups, max_step, start, unroll=2)
        for c in range(tiles):
            b = jnp.max(best[c], axis=0, keepdims=True)
            stat_send[0, :, base + c * LANES:base + (c + 1) * LANES] = b
            col[0, :, base + c * LANES:base + (c + 1) * LANES] = jnp.broadcast_to(b, (8, LANES))
            col[1, :, base + c * LANES:base + (c + 1) * LANES] = jnp.broadcast_to(
                jnp.exp2(b * alpha), (8, LANES))

    def stat_copy(step, s):
        n = 2 if step == 0 else 1
        lo = 0 if step == 0 else 1 + step
        return pltpu.make_async_remote_copy(
            stat_send.at[pl.ds(lo, n)], stat_recv.at[s, pl.ds(lo, n)],
            stat_ssem.at[step, s], stat_rsem.at[step, s],
            device_id=at(mine, lax.rem(r + s, sib)), device_id_type=pl.DeviceIdType.MESH)

    def times(x, y):
        return x * jnp.concatenate([y] * (GROUP // 8), axis=0)

    for step in range(ITERS):
        for base in range(0, cols, chunk):
            def row_step(g, _, base=base):
                acc = jnp.zeros((GROUP, LANES), F32)
                a = rows_of(top, g)
                for c in range(tiles):
                    k = mat[tile(g, base, c)]
                    if step == 0:
                        b = jnp.concatenate([lanes(col.at[0], base, c)] * (GROUP // 8), axis=0)
                        k = jnp.exp2(((k - a) - b) * alpha)
                        mat[tile(g, base, c)] = k
                    acc = acc + times(k, lanes(col.at[1], base, c))
                if base > 0:
                    acc = acc + rows_of(part, g)
                part[pl.ds(pl.multiple_of(g * GROUP, GROUP), GROUP), :] = acc
                return 0

            lax.fori_loop(0, groups, row_step, 0, unroll=2)
        total = jnp.sum(part[...], axis=1, keepdims=True)
        u_ref[...] = jnp.broadcast_to(1.0 / (total * rows_all(dims)), u_ref.shape)
        for base in range(0, cols, chunk):
            def col_step(g, acc, base=base):
                u = rows_of(u_ref, g)
                return tuple(
                    acc[c] + fold(mat[tile(g, base, c)] * u, jnp.add) for c in range(tiles))

            start = tuple(jnp.zeros((8, LANES), F32) for _ in range(tiles))
            acc = lax.fori_loop(0, groups, col_step, start, unroll=2)
            for c in range(tiles):
                stat_send[1 + step, :, base + c * LANES:base + (c + 1) * LANES] = jnp.sum(
                    acc[c], axis=0, keepdims=True)
        for s in range(1, sib):
            stat_copy(step, s).start()
        for s in range(1, sib):
            stat_copy(step, s).wait_recv()
        high = stat_send[0]
        for s in range(1, sib):
            high = jnp.maximum(high, stat_recv[s, 0])
        local = jnp.exp2((stat_send[0] - high) * alpha)
        total = local * stat_send[1 + step]
        for s in range(1, sib):
            total = total + jnp.exp2((stat_recv[s, 0] - high) * alpha) * stat_recv[s, 1 + step]
        v = local / (total * float(cols))
        col[1] = jnp.broadcast_to(v, (8, cols))

    weight_sum = weights_ref[0]
    for k in range(1, memb):
        weight_sum = weight_sum + weights_ref[k]
    weight = weights_ref[mine] / weight_sum

    def out_copy(d):
        target = peer(d)
        return pltpu.make_async_remote_copy(
            out_send.at[target], out_recv.at[mine], out_ssem.at[d], out_rsem.at[d],
            device_id=at(target, r), device_id_type=pl.DeviceIdType.MESH)

    for d in order + [0]:
        block = peer(d)

        def plan_step(g, _):
            u = rows_of(u_ref, block * (shard // GROUP) + g) * rows_all(dims)
            for base in range(0, cols, chunk):
                for c in range(tiles):
                    p = times(mat[tile(block * (shard // GROUP) + g, base, c)] * u,
                              lanes(col.at[1], base, c))
                    plan[pl.ds(pl.multiple_of(g * GROUP, GROUP), GROUP),
                         base + c * LANES:base + (c + 1) * LANES] = p.astype(BF16)
            return 0

        lax.fori_loop(0, shard // GROUP, plan_step, 0)
        term = lax.dot_general(
            plan[...], right[:dim, :], (((1,), (1,)), ((), ())), preferred_element_type=F32)
        term = jnp.transpose(term * weight)
        if d == 0:
            out_recv[mine] = term
        else:
            out_send[block] = term
            out_copy(d).start()

    for d in range(1, memb):
        out_copy(d).wait_recv()
    total = out_recv[0]
    for k in range(1, memb):
        total = total + out_recv[k]
    out_ref[...] = total

    for d in range(1, memb):
        cloud_copy(d).wait_send()
        sup_copy(d).wait_send()
        out_copy(d).wait_send()
    for s in range(1, sib):
        for d in range(memb):
            relay_copy(d, s).wait_send()
        for step in range(ITERS):
            stat_copy(step, s).wait_send()


def rows_all(dims):
    memb, sib, shard, _ = dims
    return float(memb * sib * shard)


def per_device(support, clouds, member_weights):
    devices = lax.axis_size("pts")
    memb, shard, dim = clouds.shape
    sib = devices // memb
    rows, cols = memb * shard, devices * shard
    dims = (memb, sib, shard, dim)
    vmem, dma = pltpu.VMEM, pltpu.SemaphoreType.DMA
    out = pl.pallas_call(
        functools.partial(kernel, dims),
        out_shape=jax.ShapeDtypeStruct((dim, shard), F32),
        in_specs=[
            pl.BlockSpec(memory_space=pl.ANY),
            pl.BlockSpec(memory_space=pl.ANY),
            pl.BlockSpec(memory_space=pltpu.SMEM),
        ],
        out_specs=pl.BlockSpec(memory_space=pltpu.VMEM),
        scratch_shapes=[
            vmem((memb, dim, shard), BF16),
            vmem((memb, dim, shard), BF16),
            vmem((devices, dim, shard), BF16),
            vmem((rows, dim + EXTRA), BF16),
            vmem((dim + EXTRA, cols), BF16),
            vmem((rows, cols), F32),
            vmem((rows, LANES), F32),
            vmem((rows, LANES), F32),
            vmem((rows, LANES), F32),
            vmem((2, 8, cols), F32),
            vmem((1 + ITERS, 1, cols), F32),
            vmem((sib, 1 + ITERS, 1, cols), F32),
            vmem((shard, cols), BF16),
            vmem((memb, dim, shard), F32),
            vmem((memb, dim, shard), F32),
            dma((memb,)), dma((memb,)),
            dma((memb,)), dma((memb,)),
            dma((memb, sib)), dma((memb, sib)),
            dma((ITERS, sib)), dma((ITERS, sib)),
            dma((memb,)), dma((memb,)), dma((3,)),
        ],
        compiler_params=pltpu.CompilerParams(
            collective_id=0, has_side_effects=True,
            vmem_limit_bytes=rows * cols * 4 + (16 << 20)),
    )(support.T, clouds.swapaxes(1, 2), member_weights)
    return out.T


def solution(mesh):
    in_specs = (P(("grp", "pts"), None), P(None, ("grp", "pts"), None), P("grp"))
    out_specs = P(("grp", "pts"), None)
    return jax.shard_map(
        per_device, mesh=mesh, in_specs=in_specs, out_specs=out_specs, check_vma=False
    )
```
